32 devices in a mesh: mem: 4 (over x, core), expert: 8 (over z, y).
Axes of the slice: x: 2, y: 2, z: 4, core: 2. Of those that a mesh axis runs over, the one named last changes fastest.
Arguments:
- queries: bfloat16 [8192, 4096], P(('mem', 'expert')), may hold values from -128 to 128
- out_grad: bfloat16 [8192, 4096], P(('mem', 'expert')), may hold values from -12 to 12
- mem_keys: bfloat16 [4096, 4096], P('mem', 'expert'), may hold values from -4.5 to 4.5
- mem_values: bfloat16 [4096, 4096], P('mem', 'expert'), may hold values from -48 to 48
- block_index: int32 [64, 4], P('mem'), may hold values from 0 to 31, as said below
- routes: int32 [8192, 2], P(('mem', 'expert')), may hold values from 0 to 7, all different within a row; in each aligned block of 256 rows (0 to 255, 256 to 511, ...) at most 96 rows name the same one
- combine: bfloat16 [8192, 2], P(('mem', 'expert')), may hold values from 0.049804688 to 1
- gate_pre: bfloat16 [8, 3072, 768], P('expert', 'mem'), may hold values from -6 to 6
- up_pre: bfloat16 [8, 3072, 768], P('expert', 'mem'), may hold values from -6 to 6
- w_down: bfloat16 [8, 768, 4096], P('expert', 'mem'), may hold values from -0.21875 to 0.21875
Outputs:
- query_grad: bfloat16 [8192, 4096], P('mem', 'expert')
- w_down_grad: bfloat16 [8, 768, 4096], P('expert', 'mem')
- gate_grad: bfloat16 [8, 3072, 768], P('expert', 'mem')
- up_grad: bfloat16 [8, 3072, 768], P('expert', 'mem')
- combine_grad: float32 [8, 3072], P('expert', 'mem')
The draws below stay inside these ranges and needn't reach their ends.
Inputs may be any that keep to these rules, and one draw needn't show every extreme that they name: `block_index`: each row names 4 memory blocks of 4 different owner groups, where block c belongs to group c // 8. `routes`: each row names 2 different experts; within the 256 rows of one device no expert is named by more than 96 rows, a bound that some block reaches.
All inputs are finite; a program needn't handle non-finite values.
Results may differ from the reference program's by a relative error of at most 0.013.
Values may be sent and summed in bfloat16 or wider, within the bound.
A program may use at most 192 MiB of HBM per device.

```python
import math
import jax
import jax.numpy as jnp
import numpy as np
from jax import lax

HEADS = 32
HD = 128
D = 4096
FF = 768
EXPERTS = 8
TOPK = 2
QBLK = 128
KSEL = 4
TOK_DEV = 256
MB_DEV = 8
TOKENS = 8192
NQB = 64
NMB = 32
CAP = 96
SLOTS = 3072
N_MEM = 4
N_EXPERT = 8


def draw_block_index(key, part):
    base_key = jax.random.fold_in(key, 11)
    row_keys = jax.random.split(base_key, NQB)
    owner_ids = jax.vmap(lambda row_key: jax.random.permutation(row_key, N_MEM)[:KSEL])(row_keys)
    within = jax.random.randint(jax.random.fold_in(key, 14), (NQB, KSEL), 0, MB_DEV)
    return (owner_ids * MB_DEV + within).astype(jnp.int32)


def key_rows(key):
    base_draw = jax.random.truncated_normal(jax.random.fold_in(key, 12), -4.5, 4.5, (NMB, QBLK, D), jnp.float32)
    return base_draw


def draw_mem_keys(key, part):
    return key_rows(key).reshape(NMB * QBLK, D).astype(jnp.bfloat16)


def draw_queries(key, part):
    drawn_draw = jax.random.truncated_normal(jax.random.fold_in(key, 13), -4.5, 4.5, (NQB, QBLK, D), jnp.float32)
    return drawn_draw.reshape(TOKENS, D).astype(jnp.bfloat16)


def steps_of(stream_key, extent, cuts, smallest, high):
    factor_of, own = 1.0, jax.random.fold_in(stream_key, 6)
    for axis_at, blocks in cuts:
        steps = jnp.exp(jax.random.uniform(jax.random.fold_in(own, axis_at), (blocks,), jnp.float32, smallest / len(cuts), high / len(cuts)))
        factor_of = factor_of * jnp.repeat(steps, extent[axis_at] // blocks).reshape([-1 if axis == axis_at else 1 for axis in range(len(extent))])
    return factor_of


def routed_block(stream_key, own, number, rows, number_of, top, most, lean):
    order = jax.random.permutation(stream_key, number_of)
    heavy_load, common = load_shares(number_of, rows * top, most, lean, True), load_shares(number_of, rows * top, most, lean, False)
    places = jnp.arange(number_of)

    def named(sizes, rotation):
        used = int((sizes > 0).sum())
        fixed = max(1, used // 4)
        passed = fixed + (places - fixed + rotation * (used - fixed)) % max(1, number_of - fixed)
        return jnp.zeros((number_of,), jnp.int32).at[order[jnp.where(places < fixed, places, passed)]].set(jnp.asarray(sizes, jnp.int32))

    sizes = jnp.where(number % 4 == 0, named(heavy_load, number // 4), named(common, number - number // 4 - 1))
    mixed = jax.random.permutation(jax.random.fold_in(own, 3), number_of)
    source_of, receiver = mixed[0:number_of // 2 * 2:2], mixed[1:number_of // 2 * 2:2]
    slack = jnp.minimum(sizes[source_of] - 1, most - sizes[receiver]) // 2
    slack = jnp.where((source_of == order[0]) | (receiver == order[0]) | (sizes[receiver] == 0), 0, jnp.maximum(slack, 0))
    passed = jax.random.randint(jax.random.fold_in(own, 4), (number_of // 2,), 0, 1 << 20) % (slack + 1)
    sizes = sizes.at[source_of].add(-passed).at[receiver].add(passed)
    members = jnp.searchsorted(jnp.cumsum(sizes), jnp.arange(rows * top), side="right").astype(jnp.int32)
    listing = members.reshape(top, rows).T
    listing = listing[jax.random.permutation(jax.random.fold_in(own, 1), rows)]
    rotation = jax.random.randint(jax.random.fold_in(own, 2), (rows, 1), 0, top)
    return jnp.take_along_axis(listing, (jnp.arange(top)[None, :] + rotation) % top, axis=1)


def load_shares(amount, total, most, lean, full):
    weights = [(1 << 20) // math.isqrt(rank ** lean) + 1 for rank in range(1, amount + 1)]
    largest = most if full else min(most, max(-(-total // amount), total * weights[0] // sum(weights)))
    least = 1 if total - largest >= amount - 1 else 0
    counts, rest = [largest] + [least] * (amount - 1), total - largest - least * (amount - 1)
    while rest > 0:
        movable = [i for i in range(1, amount) if counts[i] < largest] or [i for i in range(1, amount) if counts[i] < most]
        whole, remaining = sum([weights[i] for i in movable]), rest
        for i in movable:
            extra = min(most - counts[i], max(1, remaining * weights[i] // whole), rest)
            counts[i] = counts[i] + extra
            rest = rest - extra
    return np.array(counts)


def scatter_about(stream_key, shape, width, reach, cuts=(), held_as=jnp.bfloat16):
    values = jax.random.normal(stream_key, shape, jnp.float32) * width
    if len(cuts) > 0:
        values = steps_of(stream_key, shape, cuts, -0.22, 0.18) * values
    return jnp.clip(values, min=-reach, max=reach).astype(held_as)


def setup_inputs(seed: int = 0) -> dict:
    streams_of = jax.random.split(jax.random.key(seed), 11)
    queries = draw_queries(jax.random.fold_in(streams_of[10], 71), 0)
    out_grad = scatter_about(streams_of[1], (TOKENS, D), 2.0, 12.0, ((0, 32),))
    mem_keys = draw_mem_keys(jax.random.fold_in(streams_of[10], 71), 0)
    mem_values = scatter_about(streams_of[3], (NMB * QBLK, D), 8.0, 48.0, ((0, 4), (1, 8)))
    block_index = draw_block_index(jax.random.fold_in(streams_of[10], 71), 0)
    routes_keys = jax.random.split(jax.random.fold_in(streams_of[5], 1), TOKENS // TOK_DEV)
    routes_turns = jax.random.permutation(jax.random.fold_in(streams_of[5], 3), TOKENS // TOK_DEV)
    routes = jax.vmap(lambda own, number: routed_block(jax.random.fold_in(streams_of[5], 2), own, number, TOK_DEV, EXPERTS, TOPK, CAP, 2))(routes_keys, routes_turns).reshape((TOKENS, TOPK))
    combine = jnp.clip(jnp.exp(math.log(1.0) - 2.9996462 * jax.random.uniform(streams_of[6], (TOKENS, TOPK), jnp.float32) ** steps_of(streams_of[6], (TOKENS, TOPK), ((0, 32),), -0.2, 0.2)), 0.049804688, 1.0).astype(jnp.bfloat16)
    gate_pre = scatter_about(streams_of[7], (EXPERTS, SLOTS, FF), 1.0, 6.0, ((0, 8), (1, 4)))
    up_pre = scatter_about(streams_of[8], (EXPERTS, SLOTS, FF), 1.0, 6.0, ((0, 8), (1, 4)))
    w_down = scatter_about(streams_of[9], (EXPERTS, FF, D), FF ** -0.5, 0.21875, ((0, 8), (1, 4)))
    return {"queries": queries, "out_grad": out_grad, "mem_keys": mem_keys, "mem_values": mem_values, "block_index": block_index, "routes": routes, "combine": combine, "gate_pre": gate_pre, "up_pre": up_pre, "w_down": w_down}


def attend_block(inputs, keys_table, values_table):
    query_rows, grad_rows, chosen = inputs
    score_scale = 1.0 / (HD ** 0.5)
    picked_keys = keys_table[chosen].reshape(KSEL * QBLK, HEADS, HD).astype(jnp.float32)
    picked_values = values_table[chosen].reshape(KSEL * QBLK, HEADS, HD).astype(jnp.float32)
    scores = jnp.einsum("qhd,khd->hqk", query_rows.astype(jnp.float32), picked_keys) * score_scale
    highest = jnp.max(scores, axis=-1, keepdims=True)
    weights = jnp.exp(scores - highest)
    probabilities = weights / jnp.sum(weights, axis=-1, keepdims=True)
    grad_probs = jnp.einsum("qhd,khd->hqk", grad_rows.astype(jnp.float32), picked_values)
    delta_sum = jnp.sum(probabilities * grad_probs, axis=-1, keepdims=True)
    grad_scores = (probabilities * (grad_probs - delta_sum)).astype(jnp.bfloat16)
    result = jnp.einsum("hqk,khd->qhd", grad_scores.astype(jnp.float32), picked_keys) * score_scale
    return result.astype(jnp.bfloat16)


def expert_grads(inputs, out_grad):
    slot_token, slot_weight, gate_slots, up_slots, weight_rows = inputs
    present = slot_token >= 0
    slot_rows = jnp.where(present[:, None], out_grad[jnp.maximum(slot_token, 0)], jnp.zeros((), jnp.bfloat16))
    back_grad = jnp.dot(slot_rows, weight_rows.T, preferred_element_type=jnp.float32)
    gate_val = gate_slots.astype(jnp.float32)
    up_val = up_slots.astype(jnp.float32)
    sigmoid_gate = jax.nn.sigmoid(gate_val)
    silu_gate = gate_val * sigmoid_gate
    hidden = silu_gate * up_val
    combine_grad = jnp.sum(hidden * back_grad, axis=-1)
    hidden_grad = slot_weight[:, None] * back_grad
    gate_grad = (hidden_grad * up_val * sigmoid_gate * (1.0 + gate_val * (1.0 - sigmoid_gate))).astype(jnp.bfloat16)
    up_grad = (hidden_grad * silu_gate).astype(jnp.bfloat16)
    weighted = (slot_weight[:, None] * hidden).astype(jnp.bfloat16)
    group_rows = SLOTS // N_MEM
    group_terms = jnp.einsum("gsf,gsd->gfd", weighted.reshape(N_MEM, group_rows, FF).astype(jnp.float32), slot_rows.reshape(N_MEM, group_rows, D).astype(jnp.float32))
    rounded_terms = lax.optimization_barrier(group_terms.astype(jnp.bfloat16))
    down_grad = jnp.sum(rounded_terms.astype(jnp.float32), axis=0).astype(jnp.bfloat16)
    return down_grad, gate_grad, up_grad, combine_grad


def reference(queries, out_grad, mem_keys, mem_values, block_index, routes, combine, gate_pre, up_pre, w_down):
    keys_table = mem_keys.reshape(NMB, QBLK, HEADS, HD)
    values_table = mem_values.reshape(NMB, QBLK, HEADS, HD)
    query_grad = lax.map(lambda entries: attend_block(entries, keys_table, values_table), (queries.reshape(NQB, QBLK, HEADS, HD), out_grad.reshape(NQB, QBLK, HEADS, HD), block_index)).reshape(TOKENS, D)
    device_count = N_MEM * N_EXPERT
    source = routes.reshape(device_count, TOK_DEV, TOPK)
    named_count = jnp.sum((source[..., None] == jnp.arange(EXPERTS, dtype=jnp.int32)).astype(jnp.int32), axis=2, dtype=jnp.int32)
    before = jnp.cumsum(named_count, axis=1, dtype=jnp.int32) - named_count
    slot_rank = jnp.take_along_axis(before, source, axis=2).astype(jnp.int32)
    slot_index = (jnp.arange(device_count, dtype=jnp.int32)[:, None, None] * CAP + slot_rank).reshape(-1).astype(jnp.int32)
    expert_index = routes.reshape(-1).astype(jnp.int32)
    token_index = jnp.repeat(jnp.arange(TOKENS, dtype=jnp.int32), TOPK)
    slot_token = jnp.full((EXPERTS, SLOTS), -1, jnp.int32).at[expert_index, slot_index].set(token_index)
    slot_weight = jnp.zeros((EXPERTS, SLOTS), jnp.float32).at[expert_index, slot_index].set(combine.reshape(-1).astype(jnp.float32))
    down_grad, gate_grad, up_grad, combine_grad = lax.map(lambda entries: expert_grads(entries, out_grad), (slot_token, slot_weight, gate_pre, up_pre, w_down))
    return query_grad, down_grad, gate_grad, up_grad, combine_grad
```

```python
import functools

import jax
import jax.numpy as jnp
from jax import lax
from jax.experimental import pallas as pl
from jax.experimental.pallas import tpu as pltpu
from jax.sharding import PartitionSpec as P

HD = 128
QBLK = 128
DOT_NT = (((1,), (1,)), ((), ()))


def attend_kernel(idx_ref, half_ref, q_ref, near_ref, far_ref, k_ref, v_ref, o_ref):
    b = pl.program_id(0)
    side = b // (pl.num_programs(0) // 2)
    is_near = side == half_ref[0]
    ksel = idx_ref.shape[1]
    scale = 1.0 / HD**0.5
    starts = [pl.multiple_of(idx_ref[b, j] * QBLK, QBLK) for j in range(ksel)]
    for head in range(q_ref.shape[1] // HD):
        cols = slice(head * HD, (head + 1) * HD)
        q = q_ref[:, cols]
        g = jnp.where(is_near, near_ref[:, cols], far_ref[:, cols])
        k = jnp.concatenate([k_ref[pl.ds(s, QBLK), cols] for s in starts], axis=0)
        v = jnp.concatenate([v_ref[pl.ds(s, QBLK), cols] for s in starts], axis=0)
        scores = lax.dot_general(q, k, DOT_NT, preferred_element_type=jnp.float32) * scale
        grad_probs = lax.dot_general(g, v, DOT_NT, preferred_element_type=jnp.float32)
        weights = jnp.exp(scores - jnp.max(scores, axis=-1, keepdims=True))
        inverse = 1.0 / jnp.sum(weights, axis=-1, keepdims=True)
        delta = jnp.sum(weights * grad_probs, axis=-1, keepdims=True) * inverse
        grad_scores = (weights * inverse * (grad_probs - delta)).astype(jnp.bfloat16)
        out = jnp.dot(grad_scores, k, preferred_element_type=jnp.float32) * scale
        o_ref[:, cols] = out.astype(o_ref.dtype)


def attend(block_index, my_half, queries, near, far, keys, values):
    rows, width = queries.shape
    blocks = rows // QBLK
    per_side = blocks // 2

    def side_map(b, idx, half, want_near):
        mine = (b // per_side) == half[0]
        use = mine if want_near else jnp.logical_not(mine)
        return (jnp.where(use, b % per_side, 0), 0)

    whole = pl.BlockSpec(keys.shape, lambda b, *_: (0, 0), pipeline_mode=pl.Buffered(1))
    return pl.pallas_call(
        attend_kernel,
        out_shape=jax.ShapeDtypeStruct((rows, width), jnp.bfloat16),
        grid_spec=pltpu.PrefetchScalarGridSpec(
            num_scalar_prefetch=2,
            grid=(blocks,),
            in_specs=[
                pl.BlockSpec((QBLK, width), lambda b, *_: (b, 0)),
                pl.BlockSpec((QBLK, width), functools.partial(side_map, want_near=True)),
                pl.BlockSpec((QBLK, width), functools.partial(side_map, want_near=False)),
                whole,
                whole,
            ],
            out_specs=pl.BlockSpec((QBLK, width), lambda b, *_: (b, 0)),
        ),
        compiler_params=pltpu.CompilerParams(vmem_limit_bytes=40 * 2**20),
        cost_estimate=pl.CostEstimate(
            flops=6 * rows * width * block_index.shape[1] * QBLK,
            bytes_accessed=2 * (2 * keys.size + 3 * queries.size),
            transcendentals=rows * width // HD * block_index.shape[1] * QBLK,
        ),
    )(block_index, my_half, queries, near, far, keys, values)


def down_kernel(wt_ref, near_ref, far_ref, o_ref):
    cut = near_ref.shape[0]
    total = jnp.dot(wt_ref[:, :cut], near_ref[...], preferred_element_type=jnp.float32)
    total += jnp.dot(wt_ref[:, cut:], far_ref[...], preferred_element_type=jnp.float32)
    o_ref[...] = total.astype(o_ref.dtype)


def down_terms(weighted_t, near, far):
    ff, slots = weighted_t.shape
    cut, width = near.shape
    tile = min(1024, width)
    return pl.pallas_call(
        down_kernel,
        out_shape=jax.ShapeDtypeStruct((ff, width), jnp.bfloat16),
        grid=(width // tile,),
        in_specs=[
            pl.BlockSpec((ff, slots), lambda i: (0, 0)),
            pl.BlockSpec((cut, tile), lambda i: (0, i)),
            pl.BlockSpec((slots - cut, tile), lambda i: (0, i)),
        ],
        out_specs=pl.BlockSpec((ff, tile), lambda i: (0, i)),
        compiler_params=pltpu.CompilerParams(vmem_limit_bytes=40 * 2**20),
        cost_estimate=pl.CostEstimate(
            flops=2 * ff * slots * width,
            bytes_accessed=2 * (ff * slots + slots * width + ff * width),
            transcendentals=0,
        ),
    )(weighted_t, near, far)


def slot_kernel(
    half_ref, near_ref, far_ref, w_ref, gate_ref, up_ref, sw_ref, gg_ref, ug_ref, cg_ref, acc
):
    step = pl.program_id(0)
    cut = near_ref.shape[0]

    @pl.when(step == 0)
    def _():
        acc[...] = jnp.zeros_like(acc)

    w = w_ref[...]
    acc[:cut, :] += lax.dot_general(near_ref[...], w, DOT_NT, preferred_element_type=jnp.float32)
    acc[cut:, :] += lax.dot_general(far_ref[...], w, DOT_NT, preferred_element_type=jnp.float32)

    @pl.when(step == pl.num_programs(0) - 1)
    def _():
        for part in range(2):
            side = half_ref[0] if part == 0 else 1 - half_ref[0]
            rows = pl.ds(pl.multiple_of(side * cut, cut), cut)
            back = acc[part * cut : (part + 1) * cut, :]
            gate = gate_ref[rows, :].astype(jnp.float32)
            up = up_ref[rows, :].astype(jnp.float32)
            sig = jax.nn.sigmoid(gate)
            silu = gate * sig
            cg_ref[rows, :] = jnp.sum(silu * up * back, axis=-1, keepdims=True)
            hidden_grad = sw_ref[rows, :] * back
            gg_ref[rows, :] = (hidden_grad * up * sig * (1.0 + gate * (1.0 - sig))).astype(
                jnp.bfloat16
            )
            ug_ref[rows, :] = (hidden_grad * silu).astype(jnp.bfloat16)


def slot_grads(my_half, near, far, weights, gate, up, slot_weight):
    cut, width = near.shape
    slots, ff = gate.shape
    tile = min(512, width)

    def full(shape):
        return pl.BlockSpec(shape, lambda i, *_: (0, 0), pipeline_mode=pl.Buffered(1))

    return pl.pallas_call(
        slot_kernel,
        out_shape=(
            jax.ShapeDtypeStruct((slots, ff), jnp.bfloat16),
            jax.ShapeDtypeStruct((slots, ff), jnp.bfloat16),
            jax.ShapeDtypeStruct((slots, 1), jnp.float32),
        ),
        grid_spec=pltpu.PrefetchScalarGridSpec(
            num_scalar_prefetch=1,
            grid=(width // tile,),
            in_specs=[
                pl.BlockSpec((cut, tile), lambda i, *_: (0, i)),
                pl.BlockSpec((slots - cut, tile), lambda i, *_: (0, i)),
                pl.BlockSpec((ff, tile), lambda i, *_: (0, i)),
                full((slots, ff)),
                full((slots, ff)),
                full((slots, 1)),
            ],
            out_specs=(
                pl.BlockSpec((slots, ff), lambda i, *_: (0, 0)),
                pl.BlockSpec((slots, ff), lambda i, *_: (0, 0)),
                pl.BlockSpec((slots, 1), lambda i, *_: (0, 0)),
            ),
            scratch_shapes=[pltpu.VMEM((slots, ff), jnp.float32)],
        ),
        compiler_params=pltpu.CompilerParams(vmem_limit_bytes=40 * 2**20),
        cost_estimate=pl.CostEstimate(
            flops=2 * ff * slots * width,
            bytes_accessed=2 * (4 * ff * slots + slots * width + ff * width),
            transcendentals=slots * ff,
        ),
    )(my_half, near, far, weights, gate, up, slot_weight)


def before_count(hits):
    tokens = hits.shape[-1]
    earlier = jnp.triu(jnp.ones((tokens, tokens), jnp.bfloat16), 1)
    return lax.dot_general(
        hits.astype(jnp.bfloat16), earlier, (((1,), (0,)), ((), ())),
        preferred_element_type=jnp.float32,
    )


def placing_of(routes_t, experts, capacity):
    hits = jnp.any(routes_t[None, :, :] == experts[:, None, None], axis=1)
    before = before_count(hits)
    ranks = jnp.arange(capacity, dtype=jnp.float32)[None, :, None]
    placing = (before[:, None, :] == ranks) & hits[:, None, :]
    return placing.astype(jnp.bfloat16).reshape(-1, routes_t.shape[1])


def per_device(
    queries, out_grad, mem_keys, mem_values, block_index, routes, combine, gate_pre, up_pre, w_down
):
    experts = lax.axis_size("expert")
    half = experts // 2
    me = lax.axis_index("expert")
    my_half = me // half
    tokens, width = out_grad.shape
    slots, ff = gate_pre.shape[1:]
    capacity = slots // experts
    head_cols = width // experts
    groups = [list(range(half)), list(range(half, experts))]
    partner = [(i, (i + half) % experts) for i in range(experts)]

    routes_t = routes.T
    packed = jnp.concatenate([routes_t.astype(jnp.float32), combine.T.astype(jnp.float32)], axis=0)
    topk = routes_t.shape[0]

    far_grad = lax.ppermute(out_grad, "expert", partner)
    far_routes = lax.ppermute(routes_t, "expert", partner)
    packed_all = lax.all_gather(packed, "expert", axis=0, tiled=False)

    here = my_half * half + jnp.arange(half, dtype=jnp.int32)

    def exchange(rows, rows_routes):
        placing = placing_of(rows_routes, here, capacity)
        picked = jnp.dot(placing, rows, preferred_element_type=jnp.float32).astype(jnp.bfloat16)
        slot_rows = lax.all_to_all(
            picked.reshape(half, capacity, width), "expert", split_axis=0, concat_axis=0,
            axis_index_groups=groups, tiled=True,
        ).reshape(half * capacity, width)
        columns = lax.dynamic_slice_in_dim(rows, my_half * half * head_cols, half * head_cols, 1)
        columns = columns.reshape(tokens, half, head_cols).transpose(1, 0, 2)
        columns = lax.all_to_all(
            columns, "expert", split_axis=0, concat_axis=0, axis_index_groups=groups, tiled=True
        ).reshape(half * tokens, head_cols)
        return slot_rows, columns

    near_rows, near_cols = exchange(out_grad, routes_t)
    far_rows, far_cols = exchange(far_grad, far_routes)
    head_queries = lax.all_to_all(
        queries.reshape(tokens, experts, head_cols).transpose(1, 0, 2),
        "expert", split_axis=0, concat_axis=0, tiled=True,
    ).reshape(experts * tokens, head_cols)

    keys = lax.all_gather(mem_keys, "mem", axis=0, tiled=True)
    values = lax.all_gather(mem_values, "mem", axis=0, tiled=True)
    weights = lax.all_gather(w_down, "mem", axis=1, tiled=True)[0]

    named = packed_all[:, :topk, :] == me.astype(jnp.float32)
    hits = jnp.any(named, axis=1)
    token_weight = jnp.sum(jnp.where(named, packed_all[:, topk:, :], 0.0), axis=1)
    ranks = jnp.arange(capacity, dtype=jnp.float32)[None, :, None]
    filled = (before_count(hits)[:, None, :] == ranks) & hits[:, None, :]
    slot_weight = jnp.sum(jnp.where(filled, token_weight[:, None, :], 0.0), axis=2)
    slot_weight = slot_weight.reshape(slots, 1)

    gate_val = gate_pre[0].astype(jnp.float32)
    up_val = up_pre[0].astype(jnp.float32)
    weighted = (slot_weight * (gate_val * jax.nn.sigmoid(gate_val) * up_val)).astype(jnp.bfloat16)
    swapped = jnp.roll(weighted, half * capacity, axis=0)
    weighted_t = jnp.where(my_half == 0, weighted, swapped).T

    w_down_grad = lax.psum_scatter(
        down_terms(weighted_t, near_rows, far_rows), "mem", scatter_dimension=0, tiled=True
    )[None]
    side = my_half.astype(jnp.int32).reshape(1)
    query_grad = attend(block_index, side, head_queries, near_cols, far_cols, keys, values)
    gate_grad, up_grad, combine_grad = slot_grads(
        side, near_rows, far_rows, weights, gate_pre[0], up_pre[0], slot_weight
    )
    return (
        query_grad, w_down_grad, gate_grad[None], up_grad[None], combine_grad.reshape(1, slots)
    )


def solution(mesh):
    in_specs = (
        P(("mem", "expert"), None),
        P(("mem", "expert"), None),
        P("mem", "expert"),
        P("mem", "expert"),
        P("mem", None),
        P(("mem", "expert"), None),
        P(("mem", "expert"), None),
        P("expert", "mem", None),
        P("expert", "mem", None),
        P("expert", "mem", None),
    )
    out_specs = (
        P("mem", "expert"),
        P("expert", "mem", None),
        P("expert", "mem", None),
        P("expert", "mem", None),
        P("expert", "mem"),
    )
    return jax.shard_map(
        per_device, mesh=mesh, in_specs=in_specs, out_specs=out_specs, check_vma=False
    )
```

```python
import functools

import jax
import jax.numpy as jnp
from jax import lax
from jax.experimental import pallas as pl
from jax.experimental.pallas import tpu as pltpu
from jax.sharding import PartitionSpec as P


HD = 128
QBLK = 128
DOT_NT = (((1,), (1,)), ((), ()))


def attend_kernel(idx_ref, half_ref, q_ref, near_ref, far_ref, k_ref, v_ref, o_ref):
    b = pl.program_id(0)
    side = b // (pl.num_programs(0) // 2)
    is_near = side == half_ref[0]
    ksel = idx_ref.shape[1]
    scale = 1.0 / HD**0.5
    starts = [pl.multiple_of(idx_ref[b, j] * QBLK, QBLK) for j in range(ksel)]
    for head in range(q_ref.shape[1] // HD):
        cols = slice(head * HD, (head + 1) * HD)
        q = q_ref[:, cols]
        g = jnp.where(is_near, near_ref[:, cols], far_ref[:, cols])
        k = jnp.concatenate([k_ref[pl.ds(s, QBLK), cols] for s in starts], axis=0)
        v = jnp.concatenate([v_ref[pl.ds(s, QBLK), cols] for s in starts], axis=0)
        scores = lax.dot_general(q, k, DOT_NT, preferred_element_type=jnp.float32) * scale
        grad_probs = lax.dot_general(g, v, DOT_NT, preferred_element_type=jnp.float32)
        weights = jnp.exp(scores - jnp.max(scores, axis=-1, keepdims=True))
        inverse = 1.0 / jnp.sum(weights, axis=-1, keepdims=True)
        delta = jnp.sum(weights * grad_probs, axis=-1, keepdims=True) * inverse
        grad_scores = (weights * inverse * (grad_probs - delta)).astype(jnp.bfloat16)
        out = jnp.dot(grad_scores, k, preferred_element_type=jnp.float32) * scale
        o_ref[:, cols] = out.astype(o_ref.dtype)


def attend(block_index, my_half, queries, near, far, keys, values):
    rows, width = queries.shape
    blocks = rows // QBLK
    per_side = blocks // 2

    def side_map(b, idx, half, want_near):
        mine = (b // per_side) == half[0]
        use = mine if want_near else jnp.logical_not(mine)
        return (jnp.where(use, b % per_side, 0), 0)

    whole = pl.BlockSpec(keys.shape, lambda b, *_: (0, 0), pipeline_mode=pl.Buffered(1))
    return pl.pallas_call(
        attend_kernel,
        out_shape=jax.ShapeDtypeStruct((rows, width), jnp.bfloat16),
        grid_spec=pltpu.PrefetchScalarGridSpec(
            num_scalar_prefetch=2,
            grid=(blocks,),
            in_specs=[
                pl.BlockSpec((QBLK, width), lambda b, *_: (b, 0)),
                pl.BlockSpec((QBLK, width), functools.partial(side_map, want_near=True)),
                pl.BlockSpec((QBLK, width), functools.partial(side_map, want_near=False)),
                whole,
                whole,
            ],
            out_specs=pl.BlockSpec((QBLK, width), lambda b, *_: (b, 0)),
        ),
        compiler_params=pltpu.CompilerParams(vmem_limit_bytes=40 * 2**20),
        cost_estimate=pl.CostEstimate(
            flops=6 * rows * width * block_index.shape[1] * QBLK,
            bytes_accessed=2 * (2 * keys.size + 3 * queries.size),
            transcendentals=rows * width // HD * block_index.shape[1] * QBLK,
        ),
    )(block_index, my_half, queries, near, far, keys, values)


def down_kernel(wt_ref, near_ref, far_ref, o_ref):
    cut = near_ref.shape[0]
    total = jnp.dot(wt_ref[:, :cut], near_ref[...], preferred_element_type=jnp.float32)
    total += jnp.dot(wt_ref[:, cut:], far_ref[...], preferred_element_type=jnp.float32)
    o_ref[...] = total.astype(o_ref.dtype)


def down_terms(weighted_t, near, far, part):
    ff, slots = weighted_t.shape
    cut, width = far.shape
    tile = min(1024, width)
    first = part * (width // tile)
    return pl.pallas_call(
        down_kernel,
        out_shape=jax.ShapeDtypeStruct((ff, width), jnp.bfloat16),
        grid=(width // tile,),
        in_specs=[
            pl.BlockSpec((ff, slots), lambda i: (0, 0)),
            pl.BlockSpec((slots - cut, tile), lambda i: (0, i + first)),
            pl.BlockSpec((cut, tile), lambda i: (0, i)),
        ],
        out_specs=pl.BlockSpec((ff, tile), lambda i: (0, i)),
        compiler_params=pltpu.CompilerParams(vmem_limit_bytes=40 * 2**20),
        cost_estimate=pl.CostEstimate(
            flops=2 * ff * slots * width,
            bytes_accessed=2 * (ff * slots + slots * width + ff * width),
            transcendentals=0,
        ),
    )(weighted_t, near, far)


def slot_kernel(
    half_ref, near_ref, far_a_ref, far_b_ref, w_ref, gate_ref, up_ref, sw_ref, gg_ref, ug_ref, cg_ref, acc
):
    step = pl.program_id(0)
    cut = near_ref.shape[0]

    @pl.when(step == 0)
    def _():
        acc[...] = jnp.zeros_like(acc)

    w = w_ref[...]
    acc[:cut, :] += lax.dot_general(near_ref[...], w, DOT_NT, preferred_element_type=jnp.float32)
    far = jnp.where(step < pl.num_programs(0) // 2, far_a_ref[...], far_b_ref[...])
    acc[cut:, :] += lax.dot_general(far, w, DOT_NT, preferred_element_type=jnp.float32)

    @pl.when(step == pl.num_programs(0) - 1)
    def _():
        for part in range(2):
            side = half_ref[0] if part == 0 else 1 - half_ref[0]
            rows = pl.ds(pl.multiple_of(side * cut, cut), cut)
            back = acc[part * cut : (part + 1) * cut, :]
            gate = gate_ref[rows, :].astype(jnp.float32)
            up = up_ref[rows, :].astype(jnp.float32)
            sig = jax.nn.sigmoid(gate)
            silu = gate * sig
            cg_ref[rows, :] = jnp.sum(silu * up * back, axis=-1, keepdims=True)
            hidden_grad = sw_ref[rows, :] * back
            gg_ref[rows, :] = (hidden_grad * up * sig * (1.0 + gate * (1.0 - sig))).astype(
                jnp.bfloat16
            )
            ug_ref[rows, :] = (hidden_grad * silu).astype(jnp.bfloat16)


def slot_grads(my_half, near, far_a, far_b, weights, gate, up, slot_weight):
    cut, width = near.shape
    slots, ff = gate.shape
    tile = min(512, width // 2)
    per_part = width // 2 // tile

    def full(shape):
        return pl.BlockSpec(shape, lambda i, *_: (0, 0), pipeline_mode=pl.Buffered(1))

    return pl.pallas_call(
        slot_kernel,
        out_shape=(
            jax.ShapeDtypeStruct((slots, ff), jnp.bfloat16),
            jax.ShapeDtypeStruct((slots, ff), jnp.bfloat16),
            jax.ShapeDtypeStruct((slots, 1), jnp.float32),
        ),
        grid_spec=pltpu.PrefetchScalarGridSpec(
            num_scalar_prefetch=1,
            grid=(width // tile,),
            in_specs=[
                pl.BlockSpec((cut, tile), lambda i, *_: (0, i)),
                pl.BlockSpec((slots - cut, tile), lambda i, *_: (0, jnp.minimum(i, per_part - 1))),
                pl.BlockSpec((slots - cut, tile), lambda i, *_: (0, jnp.maximum(i - per_part, 0))),
                pl.BlockSpec((ff, tile), lambda i, *_: (0, i)),
                full((slots, ff)),
                full((slots, ff)),
                full((slots, 1)),
            ],
            out_specs=(
                pl.BlockSpec((slots, ff), lambda i, *_: (0, 0)),
                pl.BlockSpec((slots, ff), lambda i, *_: (0, 0)),
                pl.BlockSpec((slots, 1), lambda i, *_: (0, 0)),
            ),
            scratch_shapes=[pltpu.VMEM((slots, ff), jnp.float32)],
        ),
        compiler_params=pltpu.CompilerParams(vmem_limit_bytes=40 * 2**20),
        cost_estimate=pl.CostEstimate(
            flops=2 * ff * slots * width,
            bytes_accessed=2 * (4 * ff * slots + slots * width + ff * width),
            transcendentals=slots * ff,
        ),
    )(my_half, near, far_a, far_b, weights, gate, up, slot_weight)


def before_count(hits):
    tokens = hits.shape[-1]
    earlier = jnp.triu(jnp.ones((tokens, tokens), jnp.bfloat16), 1)
    return lax.dot_general(
        hits.astype(jnp.bfloat16), earlier, (((1,), (0,)), ((), ())),
        preferred_element_type=jnp.float32,
    )


def placing_of(routes_t, experts, capacity):
    hits = jnp.any(routes_t[None, :, :] == experts[:, None, None], axis=1)
    before = before_count(hits)
    ranks = jnp.arange(capacity, dtype=jnp.float32)[None, :, None]
    placing = (before[:, None, :] == ranks) & hits[:, None, :]
    return placing.astype(jnp.bfloat16).reshape(-1, routes_t.shape[1])


def per_device(
    queries, out_grad, mem_keys, mem_values, block_index, routes, combine, gate_pre, up_pre, w_down
):
    experts = lax.axis_size("expert")
    half = experts // 2
    me = lax.axis_index("expert")
    my_half = me // half
    tokens, width = out_grad.shape
    slots, _ = gate_pre.shape[1:]
    capacity = slots // experts
    head_cols = width // experts
    groups = [list(range(half)), list(range(half, experts))]
    partner = [(i, (i + half) % experts) for i in range(experts)]

    routes_t = routes.T
    packed = jnp.concatenate([routes_t.astype(jnp.float32), combine.T.astype(jnp.float32)], axis=0)
    topk = routes_t.shape[0]

    packed_all = lax.all_gather(packed, "expert", axis=0, tiled=False)

    def after(value, earlier):
        return lax.optimization_barrier((value, earlier))[0]

    def swap(rows, groups_used):
        return lax.all_to_all(
            rows, "expert", split_axis=0, concat_axis=0, axis_index_groups=groups_used, tiled=True
        )

    part_cols = width // 2
    far_a = lax.ppermute(after(out_grad[:, :part_cols], packed_all), "expert", partner)
    far_b = lax.ppermute(after(out_grad[:, part_cols:], far_a), "expert", partner)
    other = lax.rem(me + half, experts)
    far_routes = lax.dynamic_index_in_dim(packed_all, other, 0, keepdims=False)[:topk]
    here = my_half * half + jnp.arange(half, dtype=jnp.int32)

    def pick(placing, rows):
        picked = jnp.dot(placing, rows, preferred_element_type=jnp.float32).astype(jnp.bfloat16)
        return picked.reshape(half, capacity, rows.shape[1])

    def columns_of(rows):
        return jnp.stack([rows[:, r * head_cols : (r + 1) * head_cols] for r in range(half)])

    near_placing = placing_of(routes_t, here, capacity)
    far_placing = placing_of(far_routes, here.astype(jnp.float32), capacity)
    upper = my_half == 1
    near_own = columns_of(jnp.where(upper, out_grad[:, part_cols:], out_grad[:, :part_cols]))
    far_own = columns_of(jnp.where(upper, far_b, far_a))

    near_slots = pick(near_placing, out_grad)
    near_rows = swap(near_slots, groups)
    near_cols = swap(after(near_own, near_rows), groups)
    slots_a = after(pick(far_placing, far_a), near_cols)
    rows_a = swap(slots_a, groups)
    rows_b = swap(after(pick(far_placing, far_b), rows_a), groups)
    far_cols = swap(after(far_own, rows_b), groups)
    by_head = jnp.stack(
        [queries[:, r * head_cols : (r + 1) * head_cols] for r in range(experts)]
    )
    head_queries = swap(after(by_head, far_cols), None).reshape(experts * tokens, head_cols)
    near_rows = near_rows.reshape(half * capacity, width)
    rows_a = rows_a.reshape(half * capacity, part_cols)
    rows_b = rows_b.reshape(half * capacity, part_cols)
    near_cols = near_cols.reshape(half * tokens, head_cols)
    far_cols = far_cols.reshape(half * tokens, head_cols)

    keys = lax.all_gather(mem_keys, "mem", axis=0, tiled=True)
    values = lax.all_gather(mem_values, "mem", axis=0, tiled=True)
    weights = lax.all_gather(w_down, "mem", axis=1, tiled=True)[0]

    named = packed_all[:, :topk, :] == me.astype(jnp.float32)
    hits = jnp.any(named, axis=1)
    token_weight = jnp.sum(jnp.where(named, packed_all[:, topk:, :], 0.0), axis=1)
    ranks = jnp.arange(capacity, dtype=jnp.float32)[None, :, None]
    filled = (before_count(hits)[:, None, :] == ranks) & hits[:, None, :]
    slot_weight = jnp.sum(jnp.where(filled, token_weight[:, None, :], 0.0), axis=2)
    slot_weight = slot_weight.reshape(slots, 1)

    gate_val = gate_pre[0].astype(jnp.float32)
    up_val = up_pre[0].astype(jnp.float32)
    weighted = (slot_weight * (gate_val * jax.nn.sigmoid(gate_val) * up_val)).astype(jnp.bfloat16)
    swapped = jnp.roll(weighted, half * capacity, axis=0)
    weighted_t = jnp.where(my_half == 0, weighted, swapped).T

    down = [
        lax.psum_scatter(
            down_terms(weighted_t, near_rows, far, part), "mem", scatter_dimension=0, tiled=True
        )
        for part, far in enumerate((rows_a, rows_b))
    ]
    w_down_grad = jnp.concatenate(down, axis=1)[None]
    side = my_half.astype(jnp.int32).reshape(1)
    query_grad = attend(block_index, side, head_queries, near_cols, far_cols, keys, values)
    gate_grad, up_grad, combine_grad = slot_grads(
        side, near_rows, rows_a, rows_b, weights, gate_pre[0], up_pre[0], slot_weight
    )
    return (
        query_grad, w_down_grad, gate_grad[None], up_grad[None], combine_grad.reshape(1, slots)
    )


def solution(mesh):
    in_specs = (
        P(("mem", "expert"), None),
        P(("mem", "expert"), None),
        P("mem", "expert"),
        P("mem", "expert"),
        P("mem", None),
        P(("mem", "expert"), None),
        P(("mem", "expert"), None),
        P("expert", "mem", None),
        P("expert", "mem", None),
        P("expert", "mem", None),
    )
    out_specs = (
        P("mem", "expert"),
        P("expert", "mem", None),
        P("expert", "mem", None),
        P("expert", "mem", None),
        P("expert", "mem"),
    )

    return jax.shard_map(
        per_device, mesh=mesh, in_specs=in_specs, out_specs=out_specs, check_vma=False
    )
```

```python
import functools

import jax
import jax.numpy as jnp
from jax import lax
from jax.experimental import pallas as pl
from jax.experimental.pallas import tpu as pltpu
from jax.sharding import PartitionSpec as P


HD = 128
QBLK = 128
DOT_NT = (((1,), (1,)), ((), ()))


def attend_kernel(idx_ref, half_ref, nq_ref, fq_ref, near_ref, far_ref, k_ref, v_ref, o_ref):
    b = pl.program_id(0)
    side = b // (pl.num_programs(0) // 2)
    is_near = side == half_ref[0]
    ksel = idx_ref.shape[1]
    scale = 1.0 / HD**0.5
    starts = [pl.multiple_of(idx_ref[b, j] * QBLK, QBLK) for j in range(ksel)]
    for head in range(nq_ref.shape[1] // HD):
        cols = slice(head * HD, (head + 1) * HD)
        q = jnp.where(is_near, nq_ref[:, cols], fq_ref[:, cols])
        g = jnp.where(is_near, near_ref[:, cols], far_ref[:, cols])
        k = jnp.concatenate([k_ref[pl.ds(s, QBLK), cols] for s in starts], axis=0)
        v = jnp.concatenate([v_ref[pl.ds(s, QBLK), cols] for s in starts], axis=0)
        scores = lax.dot_general(q, k, DOT_NT, preferred_element_type=jnp.float32) * scale
        grad_probs = lax.dot_general(g, v, DOT_NT, preferred_element_type=jnp.float32)
        weights = jnp.exp(scores - jnp.max(scores, axis=-1, keepdims=True))
        inverse = 1.0 / jnp.sum(weights, axis=-1, keepdims=True)
        delta = jnp.sum(weights * grad_probs, axis=-1, keepdims=True) * inverse
        grad_scores = (weights * inverse * (grad_probs - delta)).astype(jnp.bfloat16)
        out = jnp.dot(grad_scores, k, preferred_element_type=jnp.float32) * scale
        o_ref[:, cols] = out.astype(o_ref.dtype)


def attend(block_index, my_half, near, far, tokens, keys, values):
    rows, width = near.shape
    per_source = tokens // QBLK
    blocks = rows // QBLK
    per_side = blocks // 2

    def side_map(b, idx, half, want_near, offset):
        mine = (b // per_side) == half[0]
        use = mine if want_near else jnp.logical_not(mine)
        at = jnp.where(use, b % per_side, 0)
        return (at // per_source * (2 * per_source) + at % per_source + offset, 0)

    whole = pl.BlockSpec(keys.shape, lambda b, *_: (0, 0), pipeline_mode=pl.Buffered(1))
    return pl.pallas_call(
        attend_kernel,
        out_shape=jax.ShapeDtypeStruct((rows, width), jnp.bfloat16),
        grid_spec=pltpu.PrefetchScalarGridSpec(
            num_scalar_prefetch=2,
            grid=(blocks,),
            in_specs=[
                *[
                    pl.BlockSpec(
                        (QBLK, width),
                        functools.partial(side_map, want_near=want_near, offset=offset),
                    )
                    for offset in (0, per_source)
                    for want_near in (True, False)
                ],
                whole,
                whole,
            ],
            out_specs=pl.BlockSpec((QBLK, width), lambda b, *_: (b, 0)),
        ),
        compiler_params=pltpu.CompilerParams(vmem_limit_bytes=60 * 2**20),
        cost_estimate=pl.CostEstimate(
            flops=6 * rows * width * block_index.shape[1] * QBLK,
            bytes_accessed=2 * (2 * keys.size + 3 * near.size),
            transcendentals=rows * width // HD * block_index.shape[1] * QBLK,
        ),
    )(block_index, my_half, near, far, near, far, keys, values)


def down_kernel(wt_ref, near_ref, far_ref, o_ref):
    cut = near_ref.shape[0]
    total = jnp.dot(wt_ref[:, :cut], near_ref[...], preferred_element_type=jnp.float32)
    total += jnp.dot(wt_ref[:, cut:], far_ref[...], preferred_element_type=jnp.float32)
    o_ref[...] = total.astype(o_ref.dtype)


def down_terms(weighted_t, near, far, part):
    ff, slots = weighted_t.shape
    cut, width = far.shape
    tile = min(1024, width)
    first = part * (width // tile)
    return pl.pallas_call(
        down_kernel,
        out_shape=jax.ShapeDtypeStruct((ff, width), jnp.bfloat16),
        grid=(width // tile,),
        in_specs=[
            pl.BlockSpec((ff, slots), lambda i: (0, 0)),
            pl.BlockSpec((slots - cut, tile), lambda i: (0, i + first)),
            pl.BlockSpec((cut, tile), lambda i: (0, i)),
        ],
        out_specs=pl.BlockSpec((ff, tile), lambda i: (0, i)),
        compiler_params=pltpu.CompilerParams(vmem_limit_bytes=60 * 2**20),
        cost_estimate=pl.CostEstimate(
            flops=2 * ff * slots * width,
            bytes_accessed=2 * (ff * slots + slots * width + ff * width),
            transcendentals=0,
        ),
    )(weighted_t, near, far)


def slot_kernel(
    half_ref, near_ref, far_a_ref, far_b_ref, w_ref, gate_ref, up_ref, sw_ref, gg_ref, ug_ref, cg_ref, acc
):
    step = pl.program_id(0)
    cut = near_ref.shape[0]

    @pl.when(step == 0)
    def _():
        acc[...] = jnp.zeros_like(acc)

    w = w_ref[...]
    acc[:cut, :] += lax.dot_general(near_ref[...], w, DOT_NT, preferred_element_type=jnp.float32)
    far = jnp.where(step < pl.num_programs(0) // 2, far_a_ref[...], far_b_ref[...])
    acc[cut:, :] += lax.dot_general(far, w, DOT_NT, preferred_element_type=jnp.float32)

    @pl.when(step == pl.num_programs(0) - 1)
    def _():
        for part in range(2):
            side = half_ref[0] if part == 0 else 1 - half_ref[0]
            rows = pl.ds(pl.multiple_of(side * cut, cut), cut)
            back = acc[part * cut : (part + 1) * cut, :]
            gate = gate_ref[rows, :].astype(jnp.float32)
            up = up_ref[rows, :].astype(jnp.float32)
            sig = jax.nn.sigmoid(gate)
            silu = gate * sig
            cg_ref[rows, :] = jnp.sum(silu * up * back, axis=-1, keepdims=True)
            hidden_grad = sw_ref[rows, :] * back
            gg_ref[rows, :] = (hidden_grad * up * sig * (1.0 + gate * (1.0 - sig))).astype(
                jnp.bfloat16
            )
            ug_ref[rows, :] = (hidden_grad * silu).astype(jnp.bfloat16)


def slot_grads(my_half, near, far_a, far_b, weights, gate, up, slot_weight):
    cut, width = near.shape
    slots, ff = gate.shape
    tile = min(512, width // 2)
    per_part = width // 2 // tile

    def full(shape):
        return pl.BlockSpec(shape, lambda i, *_: (0, 0), pipeline_mode=pl.Buffered(1))

    return pl.pallas_call(
        slot_kernel,
        out_shape=(
            jax.ShapeDtypeStruct((slots, ff), jnp.bfloat16),
            jax.ShapeDtypeStruct((slots, ff), jnp.bfloat16),
            jax.ShapeDtypeStruct((slots, 1), jnp.float32),
        ),
        grid_spec=pltpu.PrefetchScalarGridSpec(
            num_scalar_prefetch=1,
            grid=(width // tile,),
            in_specs=[
                pl.BlockSpec((cut, tile), lambda i, *_: (0, i)),
                pl.BlockSpec((slots - cut, tile), lambda i, *_: (0, jnp.minimum(i, per_part - 1))),
                pl.BlockSpec((slots - cut, tile), lambda i, *_: (0, jnp.maximum(i - per_part, 0))),
                pl.BlockSpec((ff, tile), lambda i, *_: (0, i)),
                full((slots, ff)),
                full((slots, ff)),
                full((slots, 1)),
            ],
            out_specs=(
                pl.BlockSpec((slots, ff), lambda i, *_: (0, 0)),
                pl.BlockSpec((slots, ff), lambda i, *_: (0, 0)),
                pl.BlockSpec((slots, 1), lambda i, *_: (0, 0)),
            ),
            scratch_shapes=[pltpu.VMEM((slots, ff), jnp.float32)],
        ),
        compiler_params=pltpu.CompilerParams(vmem_limit_bytes=60 * 2**20),
        cost_estimate=pl.CostEstimate(
            flops=2 * ff * slots * width,
            bytes_accessed=2 * (4 * ff * slots + slots * width + ff * width),
            transcendentals=slots * ff,
        ),
    )(my_half, near, far_a, far_b, weights, gate, up, slot_weight)


def before_count(hits):
    tokens = hits.shape[-1]
    earlier = jnp.triu(jnp.ones((tokens, tokens), jnp.bfloat16), 1)
    return lax.dot_general(
        hits.astype(jnp.bfloat16), earlier, (((1,), (0,)), ((), ())),
        preferred_element_type=jnp.float32,
    )


def placing_of(routes_t, experts, capacity):
    hits = jnp.any(routes_t[None, :, :] == experts[:, None, None], axis=1)
    before = before_count(hits)
    ranks = jnp.arange(capacity, dtype=jnp.float32)[None, :, None]
    placing = (before[:, None, :] == ranks) & hits[:, None, :]
    return placing.astype(jnp.bfloat16).reshape(-1, routes_t.shape[1])


def per_device(
    queries, out_grad, mem_keys, mem_values, block_index, routes, combine, gate_pre, up_pre, w_down
):
    experts = lax.axis_size("expert")
    half = experts // 2
    me = lax.axis_index("expert")
    my_half = me // half
    tokens, width = out_grad.shape
    slots, _ = gate_pre.shape[1:]
    capacity = slots // experts
    head_cols = width // experts
    groups = [list(range(half)), list(range(half, experts))]
    partner = [(i, (i + half) % experts) for i in range(experts)]

    routes_t = routes.T
    packed = jnp.concatenate([routes_t.astype(jnp.float32), combine.T.astype(jnp.float32)], axis=0)
    topk = routes_t.shape[0]

    far_routes = lax.ppermute(routes_t, "expert", partner)

    def after(value, earlier):
        return lax.optimization_barrier((value, earlier))[0]

    def swap(rows, groups_used):
        return lax.all_to_all(
            rows, "expert", split_axis=0, concat_axis=0, axis_index_groups=groups_used, tiled=True
        )

    part_cols = width // 2
    far_a = lax.ppermute(after(out_grad[:, :part_cols], far_routes), "expert", partner)
    far_b = lax.ppermute(after(out_grad[:, part_cols:], far_a), "expert", partner)
    here = my_half * half + jnp.arange(half, dtype=jnp.int32)

    def pick(placing, rows):
        picked = jnp.dot(placing, rows, preferred_element_type=jnp.float32).astype(jnp.bfloat16)
        return picked.reshape(half, capacity, rows.shape[1])

    def columns_of(rows):
        return jnp.stack([rows[:, r * head_cols : (r + 1) * head_cols] for r in range(half)])

    near_placing = placing_of(routes_t, here, capacity)
    far_placing = placing_of(far_routes, here, capacity)
    upper = my_half == 1
    low_q, high_q = queries[:, :part_cols], queries[:, part_cols:]
    far_q = lax.ppermute(
        after(jnp.where(upper, low_q, high_q), far_b), "expert", partner
    )
    own_grad = jnp.where(upper, out_grad[:, part_cols:], out_grad[:, :part_cols])
    near_own = jnp.concatenate(
        [columns_of(jnp.where(upper, high_q, low_q)), columns_of(own_grad)], axis=1
    )
    far_own = jnp.concatenate(
        [columns_of(far_q), columns_of(jnp.where(upper, far_b, far_a))], axis=1
    )

    near_slots = pick(near_placing, out_grad)
    near_rows = swap(near_slots, groups)
    packed_all = lax.all_gather(after(packed, near_slots), "expert", axis=0, tiled=False)
    near_own = after(near_own, near_rows)
    near_cols = swap(near_own, groups)
    slots_a = after(pick(far_placing, far_a), near_cols)
    rows_a = swap(slots_a, groups)
    slots_b = after(pick(far_placing, far_b), rows_a)
    rows_b = swap(slots_b, groups)
    far_cols = swap(after(far_own, rows_b), groups)
    near_rows = near_rows.reshape(half * capacity, width)
    rows_a = rows_a.reshape(half * capacity, part_cols)
    rows_b = rows_b.reshape(half * capacity, part_cols)
    near_cols = near_cols.reshape(experts * tokens, head_cols)
    far_cols = far_cols.reshape(experts * tokens, head_cols)

    keys = lax.all_gather(mem_keys, "mem", axis=0, tiled=True)
    values = lax.all_gather(mem_values, "mem", axis=0, tiled=True)
    weights = lax.all_gather(w_down, "mem", axis=1, tiled=True)[0]

    named = packed_all[:, :topk, :] == me.astype(jnp.float32)
    hits = jnp.any(named, axis=1)
    token_weight = jnp.sum(jnp.where(named, packed_all[:, topk:, :], 0.0), axis=1)
    ranks = jnp.arange(capacity, dtype=jnp.float32)[None, :, None]
    filled = (before_count(hits)[:, None, :] == ranks) & hits[:, None, :]
    slot_weight = jnp.sum(jnp.where(filled, token_weight[:, None, :], 0.0), axis=2)
    slot_weight = slot_weight.reshape(slots, 1)

    gate_val = gate_pre[0].astype(jnp.float32)
    up_val = up_pre[0].astype(jnp.float32)
    weighted = (slot_weight * (gate_val * jax.nn.sigmoid(gate_val) * up_val)).astype(jnp.bfloat16)
    swapped = jnp.roll(weighted, half * capacity, axis=0)
    weighted_t = jnp.where(my_half == 0, weighted, swapped).T

    down = [
        lax.psum_scatter(
            down_terms(weighted_t, near_rows, far, part), "mem", scatter_dimension=0, tiled=True
        )
        for part, far in enumerate((rows_a, rows_b))
    ]
    w_down_grad = jnp.concatenate(down, axis=1)[None]
    side = my_half.astype(jnp.int32).reshape(1)
    query_grad = attend(block_index, side, near_cols, far_cols, tokens, keys, values)
    gate_grad, up_grad, combine_grad = slot_grads(
        side, near_rows, rows_a, rows_b, weights, gate_pre[0], up_pre[0], slot_weight
    )
    return (
        query_grad, w_down_grad, gate_grad[None], up_grad[None], combine_grad.reshape(1, slots)
    )


def solution(mesh):
    in_specs = (
        P(("mem", "expert"), None),
        P(("mem", "expert"), None),
        P("mem", "expert"),
        P("mem", "expert"),
        P("mem", None),
        P(("mem", "expert"), None),
        P(("mem", "expert"), None),
        P("expert", "mem", None),
        P("expert", "mem", None),
        P("expert", "mem", None),
    )
    out_specs = (
        P("mem", "expert"),
        P("expert", "mem", None),
        P("expert", "mem", None),
        P("expert", "mem", None),
        P("expert", "mem"),
    )

    return jax.shard_map(
        per_device, mesh=mesh, in_specs=in_specs, out_specs=out_specs, check_vma=False
    )
```
